512 devices in a mesh: rows: 256 (over z, x_lo, y, core), cols: 2 (over x_hi).
Axes of the slice: x: 4 (x_hi: 2, x_lo: 2; x = x_hi * 2 + x_lo), y: 4, z: 16, core: 2. Of those that a mesh axis runs over, the one named last changes fastest.
Arguments:
- lower_coupling: bfloat16 [256, 1024, 1024], P('rows', 'cols'), may hold values from -0.0625 to 0.0625
- upper_coupling: bfloat16 [256, 1024, 1024], P('rows', 'cols'), may hold values from -0.0625 to 0.0625
- solution: bfloat16 [256, 1024, 256], P('rows', None, 'cols'), may hold values from -0.375 to 0.375
- cotangent: bfloat16 [256, 1024, 256], P('rows', None, 'cols'), may hold values from -6 to 6
Outputs:
- source_grad: bfloat16 [256, 1024, 256], P('rows', None, 'cols')
- lower_grad: bfloat16 [256, 1024, 1024], P('rows', 'cols')
- upper_grad: bfloat16 [256, 1024, 1024], P('rows', 'cols')
The draws below stay inside these ranges and needn't reach their ends.
All inputs are finite; a program needn't handle non-finite values.
Results may differ from the reference program's by a relative error of at most 0.0085.
Values may be sent and summed in bfloat16 or wider, within the bound.
No kernel may reach another device: no remote copies, remote signals or barrier semaphores. Data moves between devices by JAX's collectives and lax.ppermute only.
A program may use at most 64 MiB of HBM per device.

```python
import jax
import jax.numpy as jnp
import numpy as np
from jax import lax

BLOCK = 1024
ROWS = 256
COLUMNS = 256
LEVELS = 8


def level_of(stream_key, dims, pieces, least, high):
    gain, own = 1.0, jax.random.fold_in(stream_key, 6)
    for position, shards_of in pieces:
        draws = jnp.exp(jax.random.uniform(jax.random.fold_in(own, position), (shards_of,), jnp.float32, least / len(pieces), high / len(pieces)))
        gain = gain * jnp.repeat(draws, dims[position] // shards_of).reshape([-1 if axis == position else 1 for axis in range(len(dims))])
    return gain


def noise(stream_key, extent, spread, limit, pieces=(), dtype=jnp.bfloat16):
    array = spread * jax.random.normal(stream_key, extent, jnp.float32)
    if pieces:
        array = array * level_of(stream_key, extent, pieces, -0.22, 0.18)
    return jnp.clip(array, -limit, limit).astype(dtype)


def setup_inputs(seed: int = 0) -> dict:
    arg_keys = jax.random.split(jax.random.key(seed), 5)
    return {
        "lower_coupling": noise(arg_keys[0], (ROWS, BLOCK, BLOCK), (8 * BLOCK) ** -0.5, 0.0625, ((0, 256), (1, 2))),
        "upper_coupling": noise(arg_keys[1], (ROWS, BLOCK, BLOCK), (8 * BLOCK) ** -0.5, 0.0625, ((0, 256), (1, 2))),
        "solution": noise(arg_keys[2], (ROWS, BLOCK, COLUMNS), COLUMNS ** -0.5, 0.375, ((0, 256), (2, 2))),
        "cotangent": noise(arg_keys[3], (ROWS, BLOCK, COLUMNS), 1.0, 6.0, ((0, 256), (2, 2))),
    }


def reference(lower_coupling, upper_coupling, solution, cotangent):
    adjoint = cotangent.astype(jnp.float32)
    for level_no in range(LEVELS):
        stride = 2 ** level_no
        active = (np.arange(stride, ROWS, 2 * stride) + 1) % ROWS
        factor = adjoint[active].astype(jnp.bfloat16).astype(jnp.float32)
        push_down = jnp.einsum("kij,kir->kjr", lower_coupling[active].astype(jnp.float32), factor)
        push_up = jnp.einsum("kij,kir->kjr", upper_coupling[active].astype(jnp.float32), factor)
        push_down = lax.optimization_barrier(push_down.astype(jnp.bfloat16)).astype(jnp.float32)
        push_up = lax.optimization_barrier(push_up.astype(jnp.bfloat16)).astype(jnp.float32)
        adjoint = adjoint.at[(active - stride) % ROWS].add(-push_down)
        adjoint = adjoint.at[(active + stride) % ROWS].add(-push_up)
    source_grad = adjoint.astype(jnp.bfloat16)
    lower_grad = jnp.zeros((ROWS, BLOCK, BLOCK), jnp.bfloat16)
    upper_grad = jnp.zeros((ROWS, BLOCK, BLOCK), jnp.bfloat16)
    for level_no in range(LEVELS):
        stride = 2 ** level_no
        active = (np.arange(stride, ROWS, 2 * stride) + 1) % ROWS
        factor = source_grad[active].astype(jnp.float32)
        block_below = solution[(active - stride) % ROWS].astype(jnp.float32)
        block_above = solution[(active + stride) % ROWS].astype(jnp.float32)
        grad_low = -jnp.einsum("kbr,kcr->kbc", factor, block_below)
        grad_high = -jnp.einsum("kbr,kcr->kbc", factor, block_above)
        lower_grad = lower_grad.at[active].set(grad_low.astype(jnp.bfloat16))
        upper_grad = upper_grad.at[active].set(grad_high.astype(jnp.bfloat16))
    return (source_grad, lower_grad, upper_grad)
```

```python
import jax
import jax.numpy as jnp
from jax import lax
from jax.sharding import PartitionSpec as P

AXES = ("rows", "cols")
CONTRACT_FIRST = (((0,), (0,)), ((), ()))
CONTRACT_LAST = (((1,), (1,)), ((), ()))


def product(a, b, dims):
    return lax.dot_general(a, b, dims, preferred_element_type=jnp.float32)


def body(lower_coupling, upper_coupling, solution, cotangent):
    row_count = lax.axis_size("rows")
    levels = row_count.bit_length() - 1
    row = lax.axis_index("rows")
    col = lax.axis_index("cols")
    low_own, up_own = lower_coupling[0], upper_coupling[0]
    half = low_own.shape[0]
    sol_own, cot = solution[0], cotangent[0]

    def active(level):
        stride = 1 << level
        return [(o + 1) % row_count for o in range(stride, row_count, 2 * stride)]

    def flat(r, c):
        return (r % row_count) * 2 + c

    def moved(rows, shift, across=False):
        return [
            (flat(r, c), flat(r + shift, 1 - c if across else c)) for r in rows for c in range(2)
        ]

    def send(x, pairs, name):
        with jax.named_scope(name):
            return lax.ppermute(x, AXES, pairs)

    def own_rows(x):
        return lax.dynamic_slice_in_dim(x, col * half, half, 0)

    def other_rows(x):
        return lax.dynamic_slice_in_dim(x, (1 - col) * half, half, 0)

    first = active(0)
    later = [r for r in range(row_count) if r not in first]
    is_first = (row - 1) % 2 == 1
    inner = [r for r in later if r != 1]

    factor_half = jnp.concatenate([other_rows(cot), other_rows(cot)], axis=0)
    swapped = send(
        jnp.where(is_first, factor_half, sol_own), moved(range(row_count), 0, True), "swap"
    )
    low_got = send(low_own, moved(inner, 0, True), "gather_low")
    up_got = send(up_own, moved(inner, 0, True), "gather_up")

    near = own_rows(cot)
    down_near = product(low_own, near, CONTRACT_FIRST).astype(jnp.bfloat16)
    up_near = product(up_own, near, CONTRACT_FIRST).astype(jnp.bfloat16)
    a = send(up_near, moved(first, 1), "up_near")
    b = send(down_near, moved(first, -1), "down_near")
    far = swapped[:half]
    down_far = product(low_own, far, CONTRACT_FIRST).astype(jnp.bfloat16)
    up_far = product(up_own, far, CONTRACT_FIRST).astype(jnp.bfloat16)
    c = send(up_far, moved(first, 1, True), "up_far")
    d = send(down_far, moved(first, -1, True), "down_far")
    f32 = jnp.float32
    adjoint = (
        cot.astype(f32) - a.astype(f32) - b.astype(f32) - c.astype(f32) - d.astype(f32)
    )

    low = jnp.concatenate([low_own, low_got], axis=0)
    up = jnp.concatenate([up_own, up_got], axis=0)
    for level in range(1, levels):
        stride = 1 << level
        factor = adjoint.astype(jnp.bfloat16)
        ordered = jnp.concatenate([own_rows(factor), other_rows(factor)], axis=0)
        down = product(low, ordered, CONTRACT_FIRST)
        upward = product(up, ordered, CONTRACT_FIRST)
        if level < levels - 1:
            got_up = send(upward.astype(jnp.bfloat16), moved(active(level), stride), f"up{level}")
            got_down = send(down.astype(jnp.bfloat16), moved(active(level), -stride), f"down{level}")
            adjoint = adjoint - got_up.astype(f32) - got_down.astype(f32)
        else:
            both = (down + upward).astype(jnp.bfloat16)
            last = send(both, moved(active(level), stride), f"last{level}")
            final_factor = factor
            adjoint = adjoint - last.astype(f32)
    grad = adjoint.astype(jnp.bfloat16)

    sol_both = jnp.concatenate([sol_own, swapped], axis=1)
    below = above = None
    for level in range(levels):
        stride = 1 << level
        rows = active(level)
        from_below = send(sol_both, [(flat(r - stride, k), flat(r, k)) for r in rows for k in range(2)], f"below{level}")
        from_above = (
            from_below
            if level == levels - 1
            else send(sol_both, [(flat(r + stride, k), flat(r, k)) for r in rows for k in range(2)], f"above{level}")
        )
        below = from_below if below is None else below + from_below
        above = from_above if above is None else above + from_above
    theirs = send(other_rows(final_factor), moved(inner, 0, True), "swap_factor")
    theirs = jnp.where(is_first, far, theirs)
    pair = jnp.concatenate([own_rows(final_factor), theirs], axis=1)
    grad_low = -product(pair, below, CONTRACT_LAST)
    grad_high = -product(pair, above, CONTRACT_LAST)
    return (grad[None], grad_low.astype(jnp.bfloat16)[None], grad_high.astype(jnp.bfloat16)[None])


def solution(mesh):
    in_specs = (
        P("rows", "cols", None),
        P("rows", "cols", None),
        P("rows", None, "cols"),
        P("rows", None, "cols"),
    )
    out_specs = (P("rows", None, "cols"), P("rows", "cols", None), P("rows", "cols", None))
    return jax.shard_map(body, mesh=mesh, in_specs=in_specs, out_specs=out_specs, check_vma=False)
```
